32 devices in a mesh: gx: 8 (over y, x, core), gy: 4 (over z).
Axes of the slice: x: 2, y: 2, z: 4, core: 2. Of those that a mesh axis runs over, the one named last changes fastest.
Arguments:
- value_field: float32 [32, 32, 8, 1024], P('gx', 'gy'), may hold values from -6 to 6
- obstacle: float32 [32, 32, 8, 1024], P('gx', 'gy'), may hold values from -4 to 4
- drift_field: float32 [32, 32, 2], P('gx', 'gy'), may hold values from -9 to 9
Outputs:
- value_next: float32 [32, 32, 8, 1024], P('gx', 'gy')
- steps_taken: float32 [4], replicated
The draws below stay inside these ranges and needn't reach their ends.
All inputs are finite; a program needn't handle non-finite values.
Results may differ from the reference program's by a relative error of at most 0.00002.
Values sent between devices are 32-bit elements; how exact they have to be, the bound alone decides.
No kernel may reach another device: no remote copies, remote signals or barrier semaphores. Data moves between devices by JAX's collectives and lax.ppermute only.
A program may use at most 128 MiB of HBM per device.

```python
import math
import jax
import jax.numpy as jnp
from jax import lax

NTH = 8
NV = 16
NW = 64
ITERS = 4
NX = 32
NY = 32


def draw_value_field(key, part):
    extent = (NX, NY, NTH, NV * NW)
    first_pos = jnp.arange(NX).astype(jnp.float32) / max(NX - 1, 1)
    noise_field = jnp.clip(jax.random.normal(key, extent, jnp.float32), -4.0, 4.0)
    amplitude = 0.5 * 3.0 ** first_pos
    return amplitude[:, None, None, None] * noise_field


def draw_drift_field(key, part):
    extent = (NX, NY, 2)
    second_pos = jnp.arange(NY).astype(jnp.float32) / max(NY - 1, 1)
    noise_field = jnp.clip(jax.random.normal(key, extent, jnp.float32), -3.0, 3.0)
    amplitude = 0.3 * 10.0 ** second_pos
    return amplitude[None, :, None] * noise_field


def block_levels(rng, shape, cuts, least, high):
    level, own = 1.0, jax.random.fold_in(rng, 6)
    for position, shards_of in cuts:
        heights = jnp.exp(jax.random.uniform(jax.random.fold_in(own, position), (shards_of,), jnp.float32, least / len(cuts), high / len(cuts)))
        level = level * jnp.repeat(heights, shape[position] // shards_of).reshape([-1 if axis == position else 1 for axis in range(len(shape))])
    return level


def bell_draw(rng, shape, scale, bound, pieces=(), kind=jnp.bfloat16):
    result = scale * jax.random.normal(rng, shape, jnp.float32)
    if pieces:
        result = result * block_levels(rng, shape, pieces, -0.22, 0.18)
    return jnp.clip(result, -bound, bound).astype(kind)


def setup_inputs(seed: int = 0) -> dict:
    splits = jax.random.split(jax.random.key(seed), 4)
    return {
        "value_field": draw_value_field(jax.random.fold_in(splits[3], 71), 0),
        "obstacle": bell_draw(splits[1], (NX, NY, NTH, NV * NW), 1.0, 4.0, ((0, 8), (1, 4)), jnp.float32),
        "drift_field": draw_drift_field(jax.random.fold_in(splits[3], 71), 0),
    }


SPACE_STEP = 0.5
SPEED_BASE = 1.0
SPEED_STEP = 0.2
TURN_LIMIT = 0.25
EFFORT_COST = 10.0
COURANT = 0.9


def grid_lanes():
    heading = jnp.arange(NTH, dtype=jnp.int32).astype(jnp.float32) * (2.0 * math.pi / NTH)
    lane_index = jnp.arange(NV * NW, dtype=jnp.int32)
    speed_row = SPEED_BASE + (lane_index // NW).astype(jnp.float32) * SPEED_STEP
    turning = -1.0 + ((lane_index % NW).astype(jnp.float32) + 0.5) * (2.0 / NW)
    cosine_speed = jnp.cos(heading)[:, None] * speed_row[None, :]
    sine_speed = jnp.sin(heading)[:, None] * speed_row[None, :]
    return cosine_speed, sine_speed, turning


def rate_field(drift_part):
    cosine_speed, sine_speed, turning = grid_lanes()
    east_rate = cosine_speed + drift_part[:, :, 0][:, :, None, None]
    north_rate = sine_speed + drift_part[:, :, 1][:, :, None, None]
    head_step = 2.0 * math.pi / NTH
    turn_step = 2.0 / NW
    return jnp.abs(east_rate) / SPACE_STEP + jnp.abs(north_rate) / SPACE_STEP + jnp.abs(turning) / head_step + TURN_LIMIT / turn_step


def advance(extended, drift_part, barrier, time_step, slope_rate):
    center = extended[1:-1, 1:-1]
    east_plus = (extended[2:, 1:-1] - center) / SPACE_STEP
    east_minus = (center - extended[:-2, 1:-1]) / SPACE_STEP
    north_plus = (extended[1:-1, 2:] - center) / SPACE_STEP
    north_minus = (center - extended[1:-1, :-2]) / SPACE_STEP
    head_step = 2.0 * math.pi / NTH
    turn_step = 2.0 / NW
    head_plus = (jnp.roll(center, -1, axis=2) - center) / head_step
    head_minus = (center - jnp.roll(center, 1, axis=2)) / head_step
    speed_diff = (center[..., NW:] - center[..., :-NW]) / SPEED_STEP
    speed_plus = jnp.concatenate([speed_diff, speed_diff[..., -NW:]], axis=3)
    speed_minus = jnp.concatenate([speed_diff[..., :NW], speed_diff], axis=3)
    turn_diff = (center[..., 1:] - center[..., :-1]) / turn_step
    padding = jnp.zeros_like(turn_diff[..., :1])
    forward = jnp.concatenate([turn_diff, padding], axis=3)
    backward = jnp.concatenate([padding, turn_diff], axis=3)
    lane_pos = jnp.arange(center.shape[3], dtype=jnp.int32) % NW
    turn_plus = jnp.where(lane_pos == NW - 1, backward, forward)
    turn_minus = jnp.where(lane_pos == 0, forward, backward)
    cosine_speed, sine_speed, turning = grid_lanes()
    east_rate = cosine_speed + drift_part[:, :, 0][:, :, None, None]
    north_rate = sine_speed + drift_part[:, :, 1][:, :, None, None]
    speed_mean = 0.5 * (speed_plus + speed_minus)
    hamiltonian = (east_rate * (0.5 * (east_plus + east_minus))
                   + north_rate * (0.5 * (north_plus + north_minus))
                   + turning * (0.5 * (head_plus + head_minus))
                   + speed_mean * speed_mean / (2.0 * EFFORT_COST)
                   + TURN_LIMIT * jnp.abs(0.5 * (turn_plus + turn_minus)))
    damping = (jnp.abs(east_rate) * (0.5 * (east_plus - east_minus))
               + jnp.abs(north_rate) * (0.5 * (north_plus - north_minus))
               + jnp.abs(turning) * (0.5 * (head_plus - head_minus))
               + slope_rate * (0.5 * (speed_plus - speed_minus))
               + TURN_LIMIT * (0.5 * (turn_plus - turn_minus)))
    return jnp.minimum(center + time_step * (hamiltonian + damping), barrier)


def extend_edges(source, axis):
    extent = source.shape[axis]
    low_edge = 2.0 * lax.slice_in_dim(source, 0, 1, axis=axis) - lax.slice_in_dim(source, 1, 2, axis=axis)
    high_edge = 2.0 * lax.slice_in_dim(source, extent - 1, extent, axis=axis) - lax.slice_in_dim(source, extent - 2, extent - 1, axis=axis)
    return jnp.concatenate([low_edge, source, high_edge], axis=axis)


def reference(value_field, obstacle, drift_field):
    row_numbers = jnp.arange(NX, dtype=jnp.int32)

    def row_rate(row_at):
        drift_part = lax.dynamic_slice_in_dim(drift_field, row_at, 1, 0)
        return jnp.max(rate_field(drift_part))

    rate_top = jnp.max(lax.map(row_rate, row_numbers))
    step_list = []
    current_value = value_field
    for step_index in range(ITERS):
        def row_slope(row_at):
            row_data = lax.dynamic_slice_in_dim(current_value, row_at, 1, 0)
            return jnp.max(jnp.abs(row_data[..., NW:] - row_data[..., :-NW]))

        top_slope = jnp.max(lax.map(row_slope, row_numbers)) / SPEED_STEP
        rate_bound = rate_top + top_slope / (EFFORT_COST * SPEED_STEP)
        time_step = COURANT / rate_bound
        padded = extend_edges(current_value, 0)

        def row_update(row_at):
            window = extend_edges(lax.dynamic_slice_in_dim(padded, row_at, 3, 0), 1)
            drift_part = lax.dynamic_slice_in_dim(drift_field, row_at, 1, 0)
            barrier = lax.dynamic_slice_in_dim(obstacle, row_at, 1, 0)
            return advance(window, drift_part, barrier, time_step, top_slope / EFFORT_COST)[0]

        current_value = lax.map(row_update, row_numbers)
        step_list.append(time_step)
    return current_value, jnp.stack(step_list)
```

```python
import functools
import math

import jax
import jax.numpy as jnp
import numpy as np
from jax import lax
from jax.experimental import pallas as pl
from jax.experimental.pallas import tpu as pltpu
from jax.sharding import PartitionSpec as P


NTH = 8
NV = 16
NW = 64
ITERS = 4

SPACE_STEP = 0.5
SPEED_BASE = 1.0
SPEED_STEP = 0.2
TURN_LIMIT = 0.25
EFFORT_COST = 10.0
COURANT = 0.9
HEAD_STEP = 2.0 * math.pi / NTH
TURN_STEP = 2.0 / NW

LANES = 128
TILE = (NTH, LANES)
SLABS = NV * NW // LANES
VMEM_LIMIT = 24 * 1024 * 1024


def iota(dim):
    return lax.broadcasted_iota(jnp.int32, TILE, dim)


def lanes(j):
    return slice(j * LANES, (j + 1) * LANES)


def half_turn(c):
    return pltpu.roll(c, LANES // 2, axis=1)


def load(ref, *at):
    return [ref[(*at, slice(None), lanes(j))] for j in range(SLABS)]


def store(ref, cells, *at):
    for j in range(SLABS):
        ref[(*at, slice(None), lanes(j))] = cells[j]


def apart(cells, low):
    middle = SLABS // 2
    out = []
    for below, above in zip(cells[:middle], cells[middle:]):
        out += [jnp.where(low, below, half_turn(above)), jnp.where(low, half_turn(below), above)]
    return out


def together(cells, low):
    below = [jnp.where(low, c, half_turn(d)) for c, d in zip(cells[::2], cells[1::2])]
    above = [jnp.where(low, half_turn(c), d) for c, d in zip(cells[::2], cells[1::2])]
    return below + above


def speed_gap(peak, cells, low):
    for j in range(SLABS - 1):
        peak = jnp.maximum(peak, jnp.abs(cells[j + 1] - cells[j]))
    seam = jnp.abs(half_turn(cells[0]) - cells[-1])
    return jnp.maximum(peak, jnp.where(low, seam, 0.0))


def speed_sides(cells, j, low, twice):
    if j < SLABS - 1:
        after = cells[j + 1]
    else:
        after = jnp.where(low, half_turn(cells[0]), twice - cells[j - 1])
    if j:
        before = cells[j - 1]
    else:
        before = jnp.where(low, twice - cells[1], half_turn(cells[-1]))
    return after, before


def wind_at(wind, x, y):
    return wind[0, x, pl.ds(y, 1), :], wind[1, x, pl.ds(y, 1), :]


def gap_row(peak, rate_row, low):
    return jnp.where(low[:1], jnp.max(peak, keepdims=True), rate_row)


def part_sizes(bx, by):
    sizes = [by, by, bx, bx]
    return sizes + [bx * by - sum(sizes)]


def runs(bx, by):
    out, at = [], 0
    for part, size in enumerate(part_sizes(bx, by)):
        done = 0
        while done < size:
            x, y = divmod(at, by)
            length = min(size - done, by - y)
            out.append((part, done, x, y, length))
            done, at = done + length, at + length
    return out


def walk(length, width, body, carry):
    width = math.gcd(length, width)

    def trip(t, carry):
        for i in range(width):
            carry = body(t * width + i, carry)
        return carry

    return lax.fori_loop(0, length // width, trip, carry)


def fill_edges(field, near, far, low_y, high_y):
    bx, by = field.shape[:2]
    even = lax.rem(lax.axis_index("gx"), 2) == 0
    near_at = jnp.where(even, bx - 1, 0)
    far_at = jnp.where(even, 0, bx - 1)

    @pl.loop(0, by)
    def _(y):
        near[y] = field[near_at, y]
        far[y] = field[far_at, y]

    @pl.loop(0, bx)
    def _(x):
        low_y[x] = field[x, 0]
        high_y[x] = field[x, by - 1]


def first_kernel(drift, value, field, row, near, far, low_y, high_y, rate_out, table, wind, raw, sems):
    bx, by = field.shape[:2]
    copies = [pltpu.make_async_copy(value.at[x], raw.at[x], sems.at[x]) for x in range(bx)]
    for copy in copies:
        copy.start()
    low = iota(1) < NW
    heading = iota(0)
    cosine = jnp.zeros(TILE, jnp.float32)
    sine = jnp.zeros(TILE, jnp.float32)
    for a in range(NTH):
        angle = np.float32(a) * np.float32(HEAD_STEP)
        cosine = jnp.where(heading == a, np.cos(angle), cosine)
        sine = jnp.where(heading == a, np.sin(angle), sine)
    for j in range(SLABS):
        index = (j + SLABS * (iota(1) // NW)).astype(jnp.float32)
        speed = (SPEED_BASE + index * SPEED_STEP) * (1.0 / SPACE_STEP)
        table[0, :, lanes(j)] = cosine * speed
        table[1, :, lanes(j)] = sine * speed
    for x in range(bx):
        for d in range(2):
            wind[d, x] = jnp.broadcast_to(
                drift[x, :, d : d + 1] * (1.0 / SPACE_STEP), wind.shape[2:]
            )

    moving = jnp.zeros(TILE, jnp.float32)
    for x in range(bx):

        def rate_of(y, peak, x=x):
            east, north = wind_at(wind, x, y)
            for j in range(SLABS):
                peak = jnp.maximum(
                    peak,
                    jnp.abs(table[0, :, lanes(j)] + east) + jnp.abs(table[1, :, lanes(j)] + north),
                )
            return peak

        moving = walk(by, 4, rate_of, moving)
    turn = -1.0 + ((iota(1) % NW).astype(jnp.float32) + 0.5) * (2.0 / NW)
    turn_top = jnp.max(jnp.abs(turn), keepdims=True) / HEAD_STEP
    rate = jnp.max(moving, keepdims=True) + turn_top + TURN_LIMIT / TURN_STEP
    rate_row = jnp.broadcast_to(rate, (1, LANES))
    rate_out[...] = rate_row

    peak = jnp.zeros(TILE, jnp.float32)
    for x in range(bx):
        copies[x].wait()

        def gap_of(y, peak, x=x):
            cells = apart(load(raw, x, y), low)
            store(field, cells, x, y)
            return speed_gap(peak, cells, low)

        peak = walk(by, 2, gap_of, peak)
    row[...] = gap_row(peak, rate_row, low)
    fill_edges(field, near, far, low_y, high_y)


def slope_kernel(first, table, wind, near, far, from_low, from_high, center, limit, *refs):
    parts, refs = refs[:5], refs[5:]
    if first:
        barrier, kept, field, raw, sem = refs
        fetch = pltpu.make_async_copy(limit, raw, sem)
    else:
        barrier, field, sem = refs
        fetch = pltpu.make_async_copy(limit, barrier, sem)
    fetch.start()
    bx, by = center.shape[:2]
    gx, gy = lax.axis_index("gx"), lax.axis_index("gy")
    even = lax.rem(gx, 2) == 0
    near_at = jnp.where(even, bx + 1, 0)
    far_at = jnp.where(even, 0, bx + 1)

    @pl.loop(0, by)
    def _(y):
        field[near_at, y + 1] = near[y]
        field[far_at, y + 1] = far[y]
        for x in range(bx):
            field[x + 1, y + 1] = center[x, y]

    @pl.loop(0, bx)
    def _(x):
        field[x + 1, 0] = from_low[x]
        field[x + 1, by + 1] = from_high[x]

    def extend(edge, along_x, at, end, inner):
        @pl.when(edge)
        def _():
            @pl.loop(0, by if along_x else bx)
            def _(i):
                if along_x:
                    field[at, i + 1] = 2.0 * field[end, i + 1] - field[inner, i + 1]
                else:
                    field[i + 1, at] = 2.0 * field[i + 1, end] - field[i + 1, inner]

    extend(gx == 0, True, 0, 1, 2)
    extend(gx == lax.axis_size("gx") - 1, True, bx + 1, bx, bx - 1)
    extend(gy == 0, False, 0, 1, 2)
    extend(gy == lax.axis_size("gy") - 1, False, by + 1, by, by - 1)

    lane = iota(1)
    low = lane < NW
    turn = -1.0 + ((lane % NW).astype(jnp.float32) + 0.5) * (2.0 / NW)
    turn_up = turn > 0.0
    turn_rate = jnp.abs(turn) / HEAD_STEP
    turn_first = lane % NW == 0
    turn_last = lane % NW == NW - 1

    for part, start, x, y_start, length in runs(bx, by):

        def slopes(i, carry, part=part, start=start, x=x, y_start=y_start):
            y = y_start + i
            east_wind, north_wind = wind_at(wind, x, y)
            cells = load(field, x + 1, y + 1)
            for j in range(SLABS):
                c = cells[j]
                twice = c + c
                east = table[0, :, lanes(j)] + east_wind
                ahead = jnp.where(
                    east > 0.0, field[x + 2, y + 1, :, lanes(j)], field[x, y + 1, :, lanes(j)]
                )
                total = jnp.abs(east) * (ahead - c)
                north = table[1, :, lanes(j)] + north_wind
                ahead = jnp.where(
                    north > 0.0, field[x + 1, y + 2, :, lanes(j)], field[x + 1, y, :, lanes(j)]
                )
                total += jnp.abs(north) * (ahead - c)
                ahead = jnp.where(
                    turn_up, pltpu.roll(c, NTH - 1, axis=0), pltpu.roll(c, 1, axis=0)
                )
                total += turn_rate * (ahead - c)
                after = pltpu.roll(c, LANES - 1, axis=1)
                before = pltpu.roll(c, 1, axis=1)
                ahead = jnp.maximum(
                    jnp.where(turn_last, twice - before, after),
                    jnp.where(turn_first, twice - after, before),
                )
                total += (TURN_LIMIT / TURN_STEP) * (ahead - c)
                after, before = speed_sides(cells, j, low, twice)
                change = after - before
                total += (change * change) * (
                    0.25 / (SPEED_STEP * SPEED_STEP) / (2.0 * EFFORT_COST)
                )
                parts[part][start + i, :, lanes(j)] = total
            return carry

        walk(length, 2, slopes, 0)

    fetch.wait()
    if first:
        for x in range(bx):

            def rearrange(y, carry, x=x):
                store(barrier, apart(load(raw, x, y), low), x, y)
                return carry

            walk(by, 2, rearrange, 0)
        keep = pltpu.make_async_copy(barrier, kept, sem)
        keep.start()
        keep.wait()


def update_kernel(step, last, got, barrier, rate_row, steps_in, field_in, *refs):
    parts, refs = refs[:5], refs[5:]
    bx, by = field_in.shape[:2]
    lane = lax.broadcasted_iota(jnp.int32, (1, LANES), 1)
    both = jnp.max(got[...], axis=0)
    gap = jnp.max(jnp.where(lane < NW, both, 0.0), keepdims=True)
    rate = jnp.max(jnp.where(lane < NW, 0.0, both), keepdims=True)
    top_slope = gap / SPEED_STEP
    time_step = COURANT / (rate + top_slope / (EFFORT_COST * SPEED_STEP))
    weight = jnp.broadcast_to(time_step, TILE)
    weight_scaled = jnp.broadcast_to(
        time_step * (top_slope / EFFORT_COST) * (0.5 / SPEED_STEP), TILE
    )
    steps = jnp.where(lane == step, time_step, steps_in[...])
    low = iota(1) < NW
    if last:
        value_out, steps_out, field_out, sems = refs
        for i in range(ITERS):
            steps_out[i] = steps[0, i]
    else:
        field_out, near, far, low_y, high_y, row, steps_out = refs
        steps_out[...] = steps

    copies = []
    peak = jnp.zeros(TILE, jnp.float32)
    for part, start, x, y_start, length in runs(bx, by):

        def update(i, peak, part=part, start=start, x=x, y_start=y_start):
            y = y_start + i
            old = load(field_in, x, y)
            cells = []
            for j in range(SLABS):
                twice = old[j] + old[j]
                after, before = speed_sides(old, j, low, twice)
                value = old[j] + weight * parts[part][start + i, :, lanes(j)]
                value += weight_scaled * ((after + before) - twice)
                cells.append(jnp.minimum(value, barrier[x, y, :, lanes(j)]))
            if last:
                store(field_out, together(cells, low), x, y)
                return peak
            store(field_out, cells, x, y)
            return speed_gap(peak, cells, low)

        peak = walk(length, 4, update, peak)
        if last and y_start + length == by:
            copies.append(pltpu.make_async_copy(field_out.at[x], value_out.at[x], sems.at[x]))
            copies[-1].start()
    for copy in copies:
        copy.wait()
    if not last:
        row[...] = gap_row(peak, rate_row[...], low)
        fill_edges(field_out, near, far, low_y, high_y)


def hold(*arrays, space=pltpu.VMEM):
    return [pltpu.with_memory_space_constraint(a, space) for a in arrays]


def swap(cells, axis, first):
    count = lax.axis_size(axis)
    pairs = [(i, (i + 1) % count) for i in range(first, count, 2)]
    return lax.ppermute(cells, axis, pairs + [(j, i) for i, j in pairs])


def shift(cells, axis, way):
    count = lax.axis_size(axis)
    return lax.ppermute(cells, axis, [(i, (i + way) % count) for i in range(count)])


def per_device(value_field, obstacle, drift_field):
    bx, by = value_field.shape[:2]
    cells = value_field.shape[2:]
    size = value_field.size
    devices = lax.axis_size("gx") * lax.axis_size("gy")

    def in_vmem(*shape):
        return pltpu.VMEM(shape, jnp.float32)

    block = in_vmem(bx, by, *cells)
    parts = [in_vmem(n, *cells) for n in part_sizes(bx, by)]
    edges = parts[:4]
    row = in_vmem(1, LANES)
    in_hbm = jax.ShapeDtypeStruct(value_field.shape, jnp.float32)
    vmem, smem, hbm = (pl.BlockSpec(memory_space=m) for m in (pltpu.VMEM, pltpu.SMEM, pltpu.HBM))

    def call(kernel, outs, *, out_specs=None, ins, in_specs=None, scratch=(), aliases={}):
        return pl.pallas_call(
            kernel,
            out_shape=tuple(outs),
            in_specs=in_specs or [vmem] * len(ins),
            out_specs=out_specs or [vmem] * len(outs),
            scratch_shapes=scratch,
            input_output_aliases=aliases,
            compiler_params=pltpu.CompilerParams(vmem_limit_bytes=VMEM_LIMIT),
            cost_estimate=pl.CostEstimate(
                flops=40 * size, bytes_accessed=16 * size, transcendentals=0
            ),
        )(*ins)

    outs = [block, row, *edges, row, in_vmem(2, *cells), in_vmem(2, bx, by, LANES)]
    field, sent, near, far, low_y, high_y, rate_row, table, wind = call(
        first_kernel,
        outs,
        ins=[drift_field, *hold(value_field, space=pltpu.HBM)],
        in_specs=[vmem, hbm],
        scratch=[pltpu.VMEM(value_field.shape, jnp.float32), pltpu.SemaphoreType.DMA((bx,))],
    )
    steps = jnp.zeros((1, LANES), jnp.float32)
    (limit,) = hold(obstacle, space=pltpu.HBM)
    padded = pltpu.VMEM((bx + 2, by + 2, *cells), jnp.float32)

    for step in range(ITERS):
        first, last = step == 0, step == ITERS - 1
        got_edges = [
            swap(near, "gx", 0),
            swap(far, "gx", 1),
            shift(high_y, "gy", 1),
            shift(low_y, "gy", -1),
        ]
        rows = jnp.broadcast_to(sent[None], (devices, 1, LANES))
        got = lax.all_to_all(rows, ("gx", "gy"), 0, 0)
        outs = [*parts, block] + [pltpu.HBM(value_field.shape, jnp.float32)] * first
        ins = [*hold(table, wind, *got_edges, field), limit]
        result = call(
            functools.partial(slope_kernel, first),
            outs,
            out_specs=[vmem] * 6 + [hbm] * first,
            ins=ins,
            in_specs=[vmem] * 7 + [hbm],
            scratch=[padded]
            + [pltpu.VMEM(value_field.shape, jnp.float32)] * first
            + [pltpu.SemaphoreType.DMA],
            aliases={2 + i: i for i in range(4)},
        )
        slopes, barrier = result[:5], result[5]
        if first:
            (limit,) = hold(result[6], space=pltpu.HBM)
        ins = hold(got, barrier, rate_row, steps, field, *slopes)
        if last:
            return call(
                functools.partial(update_kernel, step, True),
                [in_hbm, jax.ShapeDtypeStruct((ITERS,), jnp.float32)],
                out_specs=[hbm, smem],
                ins=ins,
                scratch=[
                    pltpu.VMEM(value_field.shape, jnp.float32),
                    pltpu.SemaphoreType.DMA((bx,)),
                ],
            )
        field, near, far, low_y, high_y, sent, steps = call(
            functools.partial(update_kernel, step, False),
            [block, *edges, row, row],
            ins=ins,
            aliases={4: 0, **{5 + i: 1 + i for i in range(4)}},
        )


def solution(mesh):
    return jax.shard_map(
        per_device,
        mesh=mesh,
        in_specs=(P("gx", "gy", None, None), P("gx", "gy", None, None), P("gx", "gy", None)),
        out_specs=(P("gx", "gy", None, None), P()),
        check_vma=False,
    )
```

```python
import functools
import math

import jax
import jax.numpy as jnp
import numpy as np
from jax import lax
from jax.experimental import pallas as pl
from jax.experimental.pallas import tpu as pltpu
from jax.sharding import PartitionSpec as P


NTH = 8
NV = 16
NW = 64
ITERS = 4

SPACE_STEP = 0.5
SPEED_BASE = 1.0
SPEED_STEP = 0.2
TURN_LIMIT = 0.25
EFFORT_COST = 10.0
COURANT = 0.9
HEAD_STEP = 2.0 * math.pi / NTH
TURN_STEP = 2.0 / NW

LANES = 128
TILE = (NTH, LANES)
SLABS = NV * NW // LANES
VMEM_LIMIT = 24 * 1024 * 1024


def iota(dim):
    return lax.broadcasted_iota(jnp.int32, TILE, dim)


def lanes(j):
    return slice(j * LANES, (j + 1) * LANES)


def half_turn(c):
    return pltpu.roll(c, LANES // 2, axis=1)


def load(ref, *at):
    return [ref[(*at, slice(None), lanes(j))] for j in range(SLABS)]


def store(ref, cells, *at):
    for j in range(SLABS):
        ref[(*at, slice(None), lanes(j))] = cells[j]


def apart(cells, low):
    middle = SLABS // 2
    out = []
    for below, above in zip(cells[:middle], cells[middle:]):
        out += [jnp.where(low, below, half_turn(above)), jnp.where(low, half_turn(below), above)]
    return out


def together(cells, low):
    below = [jnp.where(low, c, half_turn(d)) for c, d in zip(cells[::2], cells[1::2])]
    above = [jnp.where(low, half_turn(c), d) for c, d in zip(cells[::2], cells[1::2])]
    return below + above


def speed_gap(peak, cells, low):
    for j in range(SLABS - 1):
        peak = jnp.maximum(peak, jnp.abs(cells[j + 1] - cells[j]))
    seam = jnp.abs(half_turn(cells[0]) - cells[-1])
    return jnp.maximum(peak, jnp.where(low, seam, 0.0))


def speed_sides(cells, j, low, twice):
    if j < SLABS - 1:
        after = cells[j + 1]
    else:
        after = jnp.where(low, half_turn(cells[0]), twice - cells[j - 1])
    if j:
        before = cells[j - 1]
    else:
        before = jnp.where(low, twice - cells[1], half_turn(cells[-1]))
    return after, before


def wind_at(wind, x, y):
    return wind[0, x, y : y + 1, :], wind[1, x, y : y + 1, :]


def gap_row(peak, rate_row, low):
    return jnp.where(low[:1], jnp.max(peak, keepdims=True), rate_row)


def part_sizes(bx, by):
    sizes = [by, by, bx, bx]
    return sizes + [bx * by - sum(sizes)]


def runs(bx, by):
    out, at = [], 0
    for part, size in enumerate(part_sizes(bx, by)):
        done = 0
        while done < size:
            x, y = divmod(at, by)
            length = min(size - done, by - y)
            out.append((part, done, x, y, length))
            done, at = done + length, at + length
    return out


def walk(length, body, carry):
    for i in range(length):
        carry = body(i, carry)
    return carry


def fill_edges(field, near_x, far_x, near_y, far_y):
    bx, by = field.shape[:2]
    for axis, size, near, far in (("gx", bx, near_x, far_x), ("gy", by, near_y, far_y)):
        even = lax.rem(lax.axis_index(axis), 2) == 0
        near_at = jnp.where(even, size - 1, 0)
        far_at = jnp.where(even, 0, size - 1)
        for i in range(near.shape[0]):
            near[i] = field[near_at, i] if axis == "gx" else field[i, near_at]
            far[i] = field[far_at, i] if axis == "gx" else field[i, far_at]


def first_kernel(drift_in, value, field, row, near_x, far_x, near_y, far_y, rate_out, table, wind, raw, drift, sems):
    bx, by = field.shape[:2]
    copies = [pltpu.make_async_copy(value.at[x], raw.at[x], sems.at[x]) for x in range(bx)]
    copies.append(pltpu.make_async_copy(drift_in, drift, sems.at[bx]))
    for copy in copies[-1:] + copies[:-1]:
        copy.start()
    low = iota(1) < NW
    heading = iota(0)
    cosine = jnp.zeros(TILE, jnp.float32)
    sine = jnp.zeros(TILE, jnp.float32)
    for a in range(NTH):
        angle = np.float32(a) * np.float32(HEAD_STEP)
        cosine = jnp.where(heading == a, np.cos(angle), cosine)
        sine = jnp.where(heading == a, np.sin(angle), sine)
    for j in range(SLABS):
        index = (j + SLABS * (iota(1) // NW)).astype(jnp.float32)
        speed = (SPEED_BASE + index * SPEED_STEP) * (1.0 / SPACE_STEP)
        table[0, :, lanes(j)] = cosine * speed
        table[1, :, lanes(j)] = sine * speed
    copies[bx].wait()
    diagonal = lax.broadcasted_iota(jnp.int32, (by, by), 0) == lax.broadcasted_iota(
        jnp.int32, (by, by), 1
    )
    for x in range(bx):
        for d in range(2):
            square = jnp.broadcast_to(drift[x, d : d + 1, :] * (1.0 / SPACE_STEP), (by, by))
            column = jnp.sum(jnp.where(diagonal, square, 0.0), axis=1, keepdims=True)
            wind[d, x] = jnp.broadcast_to(column, wind.shape[2:])

    moving = jnp.zeros(TILE, jnp.float32)
    for x in range(bx):

        def rate_of(y, peak, x=x):
            east, north = wind_at(wind, x, y)
            for j in range(SLABS):
                peak = jnp.maximum(
                    peak,
                    jnp.abs(table[0, :, lanes(j)] + east) + jnp.abs(table[1, :, lanes(j)] + north),
                )
            return peak

        moving = walk(by, rate_of, moving)
    turn = -1.0 + ((iota(1) % NW).astype(jnp.float32) + 0.5) * (2.0 / NW)
    turn_top = jnp.max(jnp.abs(turn), keepdims=True) / HEAD_STEP
    rate = jnp.max(moving, keepdims=True) + turn_top + TURN_LIMIT / TURN_STEP
    rate_row = jnp.broadcast_to(rate, (1, LANES))
    rate_out[...] = rate_row

    peak = jnp.zeros(TILE, jnp.float32)
    for x in range(bx):
        copies[x].wait()

        def gap_of(y, peak, x=x):
            cells = apart(load(raw, x, y), low)
            store(field, cells, x, y)
            return speed_gap(peak, cells, low)

        peak = walk(by, gap_of, peak)
    row[...] = gap_row(peak, rate_row, low)
    fill_edges(field, near_x, far_x, near_y, far_y)


def slope_kernel(first, table, wind, near_x, far_x, near_y, far_y, center, limit, *refs):
    parts, refs = refs[:5], refs[5:]
    bx, by = center.shape[:2]
    barrier, refs = refs[:bx], refs[bx:]
    if first:
        kept, field, raw, sems = refs
        targets = [raw.at[x] for x in range(bx)]
    else:
        field, sems = refs
        targets = barrier
    fetches = [pltpu.make_async_copy(limit.at[x], targets[x], sems.at[x]) for x in range(bx)]
    for fetch in fetches:
        fetch.start()
    gx, gy = lax.axis_index("gx"), lax.axis_index("gy")
    for x in range(bx):
        for y in range(by):
            field[x + 1, y + 1] = center[x, y]
    for index, size, near, far in ((gx, bx, near_x, far_x), (gy, by, near_y, far_y)):
        even = lax.rem(index, 2) == 0
        near_at = jnp.where(even, size + 1, 0)
        far_at = jnp.where(even, 0, size + 1)
        for i in range(near.shape[0]):
            if near is near_x:
                field[near_at, i + 1] = near[i]
                field[far_at, i + 1] = far[i]
            else:
                field[i + 1, near_at] = near[i]
                field[i + 1, far_at] = far[i]

    def extend(edge, along_x, at, end, inner):
        @pl.when(edge)
        def _():
            for i in range(1, (by if along_x else bx) + 1):
                if along_x:
                    field[at, i] = 2.0 * field[end, i] - field[inner, i]
                else:
                    field[i, at] = 2.0 * field[i, end] - field[i, inner]

    extend(gx == 0, True, 0, 1, 2)
    extend(gx == lax.axis_size("gx") - 1, True, bx + 1, bx, bx - 1)
    extend(gy == 0, False, 0, 1, 2)
    extend(gy == lax.axis_size("gy") - 1, False, by + 1, by, by - 1)

    lane = iota(1)
    low = lane < NW
    turn = -1.0 + ((lane % NW).astype(jnp.float32) + 0.5) * (2.0 / NW)
    turn_up = turn > 0.0
    turn_rate = jnp.abs(turn) / HEAD_STEP
    turn_first = lane % NW == 0
    turn_last = lane % NW == NW - 1

    for part, start, x, y_start, length in runs(bx, by):

        def slopes(i, carry, part=part, start=start, x=x, y_start=y_start):
            y = y_start + i
            east_wind, north_wind = wind_at(wind, x, y)
            cells = load(field, x + 1, y + 1)
            for j in range(SLABS):
                c = cells[j]
                twice = c + c
                east = table[0, :, lanes(j)] + east_wind
                ahead = jnp.where(
                    east > 0.0, field[x + 2, y + 1, :, lanes(j)], field[x, y + 1, :, lanes(j)]
                )
                total = jnp.abs(east) * (ahead - c)
                north = table[1, :, lanes(j)] + north_wind
                ahead = jnp.where(
                    north > 0.0, field[x + 1, y + 2, :, lanes(j)], field[x + 1, y, :, lanes(j)]
                )
                total += jnp.abs(north) * (ahead - c)
                ahead = jnp.where(
                    turn_up, pltpu.roll(c, NTH - 1, axis=0), pltpu.roll(c, 1, axis=0)
                )
                total += turn_rate * (ahead - c)
                after = pltpu.roll(c, LANES - 1, axis=1)
                before = pltpu.roll(c, 1, axis=1)
                ahead = jnp.maximum(
                    jnp.where(turn_last, twice - before, after),
                    jnp.where(turn_first, twice - after, before),
                )
                total += (TURN_LIMIT / TURN_STEP) * (ahead - c)
                after, before = speed_sides(cells, j, low, twice)
                change = after - before
                total += (change * change) * (
                    0.25 / (SPEED_STEP * SPEED_STEP) / (2.0 * EFFORT_COST)
                )
                parts[part][start + i, :, lanes(j)] = total
            return carry

        walk(length, slopes, 0)

    for fetch in fetches:
        fetch.wait()
    if first:
        keeps = []
        for x in range(bx):
            for y in range(by):
                store(barrier[x], apart(load(raw, x, y), low), y)
            keeps.append(pltpu.make_async_copy(barrier[x], kept.at[x], sems.at[x]))
            keeps[-1].start()
        for keep in keeps:
            keep.wait()


def update_kernel(step, last, got, rate_row, steps_in, field_in, *refs):
    bx, by = field_in.shape[:2]
    parts, barrier, refs = refs[:5], refs[5 : 5 + bx], refs[5 + bx :]
    lane = lax.broadcasted_iota(jnp.int32, (1, LANES), 1)
    both = jnp.max(got[...], axis=0)
    gap = jnp.max(jnp.where(lane < NW, both, 0.0), keepdims=True)
    rate = jnp.max(jnp.where(lane < NW, 0.0, both), keepdims=True)
    top_slope = gap / SPEED_STEP
    time_step = COURANT / (rate + top_slope / (EFFORT_COST * SPEED_STEP))
    weight = jnp.broadcast_to(time_step, TILE)
    weight_scaled = jnp.broadcast_to(
        time_step * (top_slope / EFFORT_COST) * (0.5 / SPEED_STEP), TILE
    )
    steps = jnp.where(lane == step, time_step, steps_in[...])
    low = iota(1) < NW
    if last:
        value_out, steps_out, field_out, steps_here, sems = refs
    else:
        field_out, near_x, far_x, near_y, far_y, row, steps_out = refs
        steps_out[...] = steps

    copies = []
    if last:
        for i in range(ITERS):
            steps_here[i] = steps[0, i]
        copies.append(pltpu.make_async_copy(steps_here, steps_out, sems.at[bx]))
        copies[0].start()
    peak = jnp.zeros(TILE, jnp.float32)
    for part, start, x, y_start, length in runs(bx, by):

        def update(i, peak, part=part, start=start, x=x, y_start=y_start):
            y = y_start + i
            old = load(field_in, x, y)
            cells = []
            for j in range(SLABS):
                twice = old[j] + old[j]
                after, before = speed_sides(old, j, low, twice)
                value = old[j] + weight * parts[part][start + i, :, lanes(j)]
                value += weight_scaled * ((after + before) - twice)
                cells.append(jnp.minimum(value, barrier[x][y, :, lanes(j)]))
            if last:
                store(field_out, together(cells, low), x, y)
                return peak
            store(field_out, cells, x, y)
            return speed_gap(peak, cells, low)

        peak = walk(length, update, peak)
        if last and y_start + length == by:
            copies.append(pltpu.make_async_copy(field_out.at[x], value_out.at[x], sems.at[x]))
            copies[-1].start()
    if last:
        for copy in copies:
            copy.wait()
    else:
        row[...] = gap_row(peak, rate_row[...], low)
        fill_edges(field_out, near_x, far_x, near_y, far_y)


def hold(*arrays, space=pltpu.VMEM):
    return [pltpu.with_memory_space_constraint(a, space) for a in arrays]


def swap(cells, along, first):
    nx, ny = lax.axis_size("gx"), lax.axis_size("gy")
    pairs = []
    for x in range(nx):
        for y in range(ny):
            if along == "gx":
                if (x - first) % 2 == 0 and (x + 1 < nx or first):
                    pairs.append(((x, y), ((x + 1) % nx, y)))
            elif y >= first and (y - first) % 2 == 0 and y + 1 < ny:
                pairs.append(((x, y), (x, y + 1)))
    paired = {i for pair in pairs for i in pair}
    for x in range(0, nx - 1, 2):
        for y in range(ny):
            if not paired & {(x, y), (x + 1, y)}:
                pairs.append(((x, y), (x + 1, y)))
    links = [(i * ny + j, k * ny + m) for (i, j), (k, m) in pairs]
    return lax.ppermute(cells, ("gx", "gy"), links + [(j, i) for i, j in links])


def per_device(value_field, obstacle, drift_field):
    bx, by = value_field.shape[:2]
    cells = value_field.shape[2:]
    size = value_field.size
    devices = lax.axis_size("gx") * lax.axis_size("gy")

    def in_vmem(*shape):
        return pltpu.VMEM(shape, jnp.float32)

    block = in_vmem(bx, by, *cells)
    parts = [in_vmem(n, *cells) for n in part_sizes(bx, by)]
    edges = parts[:4]
    row = in_vmem(1, LANES)
    in_hbm = jax.ShapeDtypeStruct(value_field.shape, jnp.float32)
    vmem, _, hbm = (pl.BlockSpec(memory_space=m) for m in (pltpu.VMEM, pltpu.SMEM, pltpu.HBM))

    def call(kernel, outs, *, out_specs=None, ins, in_specs=None, scratch=(), aliases={}):
        return pl.pallas_call(
            kernel,
            out_shape=tuple(outs),
            in_specs=in_specs or [vmem] * len(ins),
            out_specs=out_specs or [vmem] * len(outs),
            scratch_shapes=scratch,
            input_output_aliases=aliases,
            compiler_params=pltpu.CompilerParams(vmem_limit_bytes=VMEM_LIMIT),
            cost_estimate=pl.CostEstimate(
                flops=40 * size, bytes_accessed=16 * size, transcendentals=0
            ),
        )(*ins)

    outs = [block, row, *edges, row, in_vmem(2, *cells), in_vmem(2, bx, by, LANES)]
    field, sent, near_x, far_x, near_y, far_y, rate_row, table, wind = call(
        first_kernel,
        outs,
        ins=hold(drift_field.transpose(0, 2, 1), value_field, space=pltpu.HBM),
        in_specs=[hbm, hbm],
        scratch=[
            pltpu.VMEM(value_field.shape, jnp.float32),
            pltpu.VMEM((bx, 2, by), jnp.float32),
            pltpu.SemaphoreType.DMA((bx + 1,)),
        ],
    )
    steps = jnp.zeros((1, LANES), jnp.float32)
    (limit,) = hold(obstacle, space=pltpu.HBM)
    padded = pltpu.VMEM((bx + 2, by + 2, *cells), jnp.float32)

    for step in range(ITERS):
        first, last = step == 0, step == ITERS - 1
        got_far_x = swap(far_x, "gx", 1)
        got_near_y = swap(near_y, "gy", 0)
        got_far_y = swap(far_y, "gy", 1)
        got_near_x = swap(near_x, "gx", 0)
        got_edges = [got_near_x, got_far_x, got_near_y, got_far_y]
        rows = jnp.broadcast_to(sent[None], (devices, 1, LANES))
        got = lax.all_to_all(rows, ("gx", "gy"), 0, 0)
        outs = [*parts, *[in_vmem(by, *cells)] * bx] + [pltpu.HBM(value_field.shape, jnp.float32)] * first
        ins = [*hold(table, wind, *got_edges, field), limit]
        result = call(
            functools.partial(slope_kernel, first),
            outs,
            out_specs=[vmem] * (5 + bx) + [hbm] * first,
            ins=ins,
            in_specs=[vmem] * 7 + [hbm],
            scratch=[padded]
            + [pltpu.VMEM(value_field.shape, jnp.float32)] * first
            + [pltpu.SemaphoreType.DMA((bx,))],
            aliases={2 + i: i for i in range(4)},
        )
        if first:
            *result, limit = result
            (limit,) = hold(limit, space=pltpu.HBM)
        ins = hold(got, rate_row, steps, field, *result)
        if last:
            return call(
                functools.partial(update_kernel, step, True),
                [in_hbm, jax.ShapeDtypeStruct((ITERS,), jnp.float32)],
                out_specs=[hbm, hbm],
                ins=ins,
                scratch=[
                    pltpu.VMEM(value_field.shape, jnp.float32),
                    pltpu.SMEM((ITERS,), jnp.float32),
                    pltpu.SemaphoreType.DMA((bx + 1,)),
                ],
            )
        field, near_x, far_x, near_y, far_y, sent, steps = call(
            functools.partial(update_kernel, step, False),
            [block, *edges, row, row],
            ins=ins,
            aliases={3: 0, **{4 + i: 1 + i for i in range(4)}},
        )


def solution(mesh):
    return jax.shard_map(
        per_device,
        mesh=mesh,
        in_specs=(P("gx", "gy", None, None), P("gx", "gy", None, None), P("gx", "gy", None)),
        out_specs=(P("gx", "gy", None, None), P()),
        check_vma=False,
    )
```

```python
import functools
import math

import jax
import jax.numpy as jnp
import numpy as np
from jax import lax
from jax.experimental import pallas as pl
from jax.experimental.pallas import tpu as pltpu
from jax.sharding import PartitionSpec as P


NTH = 8
NV = 16
NW = 64
ITERS = 4

SPACE_STEP = 0.5
SPEED_BASE = 1.0
SPEED_STEP = 0.2
TURN_LIMIT = 0.25
EFFORT_COST = 10.0
COURANT = 0.9
HEAD_STEP = 2.0 * math.pi / NTH
TURN_STEP = 2.0 / NW

LANES = 128
TILE = (NTH, LANES)
SLABS = NV * NW // LANES
VMEM_LIMIT = 24 * 1024 * 1024


def iota(dim):
    return lax.broadcasted_iota(jnp.int32, TILE, dim)


def lanes(j):
    return slice(j * LANES, (j + 1) * LANES)


def half_turn(c):
    return pltpu.roll(c, LANES // 2, axis=1)


def load(ref, *at):
    return [ref[(*at, slice(None), lanes(j))] for j in range(SLABS)]


def store(ref, cells, *at):
    for j in range(SLABS):
        ref[(*at, slice(None), lanes(j))] = cells[j]


def apart(cells, low):
    middle = SLABS // 2
    out = []
    for below, above in zip(cells[:middle], cells[middle:]):
        out += [jnp.where(low, below, half_turn(above)), jnp.where(low, half_turn(below), above)]
    return out


def together(cells, low):
    below = [jnp.where(low, c, half_turn(d)) for c, d in zip(cells[::2], cells[1::2])]
    above = [jnp.where(low, half_turn(c), d) for c, d in zip(cells[::2], cells[1::2])]
    return below + above


def speed_gap(peak, cells, low):
    for j in range(SLABS - 1):
        peak = jnp.maximum(peak, jnp.abs(cells[j + 1] - cells[j]))
    seam = jnp.abs(half_turn(cells[0]) - cells[-1])
    return jnp.maximum(peak, jnp.where(low, seam, 0.0))


def speed_sides(cells, j, low, twice):
    if j < SLABS - 1:
        after = cells[j + 1]
    else:
        after = jnp.where(low, half_turn(cells[0]), twice - cells[j - 1])
    if j:
        before = cells[j - 1]
    else:
        before = jnp.where(low, twice - cells[1], half_turn(cells[-1]))
    return after, before


def wind_at(wind, x, y):
    return wind[0, x, y : y + 1, :], wind[1, x, y : y + 1, :]


def gap_row(peak, rate_row, low):
    return jnp.where(low[:1], jnp.max(peak, keepdims=True), rate_row)


def part_sizes(bx, by):
    sizes = [by, by, bx, bx]
    return sizes + [bx * by - sum(sizes)]


def runs(bx, by):
    out, at = [], 0
    for part, size in enumerate(part_sizes(bx, by)):
        done = 0
        while done < size:
            x, y = divmod(at, by)
            length = min(size - done, by - y)
            out.append((part, done, x, y, length))
            done, at = done + length, at + length
    return out


def walk(length, body, carry):
    for i in range(length):
        carry = body(i, carry)
    return carry


def fill_edges(field, near_x, far_x, near_y, far_y):
    bx, by = field.shape[:2]
    for axis, size, near, far in (("gx", bx, near_x, far_x), ("gy", by, near_y, far_y)):
        even = lax.rem(lax.axis_index(axis), 2) == 0
        near_at = jnp.where(even, size - 1, 0)
        far_at = jnp.where(even, 0, size - 1)
        for i in range(near.shape[0]):
            near[i] = field[near_at, i] if axis == "gx" else field[i, near_at]
            far[i] = field[far_at, i] if axis == "gx" else field[i, far_at]


def first_kernel(drift_in, value, field, row, near_x, far_x, near_y, far_y, rate_out, table, wind, raw, drift, sems):
    bx, by = field.shape[:2]
    copies = [pltpu.make_async_copy(value.at[x], raw.at[x], sems.at[x]) for x in range(bx)]
    copies.append(pltpu.make_async_copy(drift_in, drift, sems.at[bx]))
    for copy in copies[-1:] + copies[:-1]:
        copy.start()
    low = iota(1) < NW
    heading = iota(0)
    cosine = jnp.zeros(TILE, jnp.float32)
    sine = jnp.zeros(TILE, jnp.float32)
    for a in range(NTH):
        angle = np.float32(a) * np.float32(HEAD_STEP)
        cosine = jnp.where(heading == a, np.cos(angle), cosine)
        sine = jnp.where(heading == a, np.sin(angle), sine)
    for j in range(SLABS):
        index = (j + SLABS * (iota(1) // NW)).astype(jnp.float32)
        speed = (SPEED_BASE + index * SPEED_STEP) * (1.0 / SPACE_STEP)
        table[0, :, lanes(j)] = cosine * speed
        table[1, :, lanes(j)] = sine * speed
    copies[bx].wait()
    diagonal = lax.broadcasted_iota(jnp.int32, (by, by), 0) == lax.broadcasted_iota(
        jnp.int32, (by, by), 1
    )
    for x in range(bx):
        for d in range(2):
            square = jnp.broadcast_to(drift[x, d : d + 1, :] * (1.0 / SPACE_STEP), (by, by))
            column = jnp.sum(jnp.where(diagonal, square, 0.0), axis=1, keepdims=True)
            wind[d, x] = jnp.broadcast_to(column, wind.shape[2:])

    moving = jnp.zeros(TILE, jnp.float32)
    for x in range(bx):

        def rate_of(y, peak, x=x):
            east, north = wind_at(wind, x, y)
            for j in range(SLABS):
                peak = jnp.maximum(
                    peak,
                    jnp.abs(table[0, :, lanes(j)] + east) + jnp.abs(table[1, :, lanes(j)] + north),
                )
            return peak

        moving = walk(by, rate_of, moving)
    turn = -1.0 + ((iota(1) % NW).astype(jnp.float32) + 0.5) * (2.0 / NW)
    turn_top = jnp.max(jnp.abs(turn), keepdims=True) / HEAD_STEP
    rate = jnp.max(moving, keepdims=True) + turn_top + TURN_LIMIT / TURN_STEP
    rate_row = jnp.broadcast_to(rate, (1, LANES))
    rate_out[...] = rate_row

    peak = jnp.zeros(TILE, jnp.float32)
    for x in range(bx):
        copies[x].wait()

        def gap_of(y, peak, x=x):
            cells = apart(load(raw, x, y), low)
            store(field, cells, x, y)
            return speed_gap(peak, cells, low)

        peak = walk(by, gap_of, peak)
    row[...] = gap_row(peak, rate_row, low)
    fill_edges(field, near_x, far_x, near_y, far_y)


def slope_kernel(first, table, wind, near_x, far_x, near_y, far_y, center, limit, *refs):
    parts, refs = refs[:5], refs[5:]
    bx, by = center.shape[:2]
    barrier, refs = refs[:bx], refs[bx:]
    if first:
        kept, field, raw, sems = refs
        targets = [raw.at[x] for x in range(bx)]
    else:
        field, sems = refs
        targets = barrier
    fetches = [pltpu.make_async_copy(limit.at[x], targets[x], sems.at[x]) for x in range(bx)]
    for fetch in fetches:
        fetch.start()
    gx, gy = lax.axis_index("gx"), lax.axis_index("gy")
    for x in range(bx):
        for y in range(by):
            field[x + 1, y + 1] = center[x, y]
    for index, size, near, far in ((gx, bx, near_x, far_x), (gy, by, near_y, far_y)):
        even = lax.rem(index, 2) == 0
        near_at = jnp.where(even, size + 1, 0)
        far_at = jnp.where(even, 0, size + 1)
        for i in range(near.shape[0]):
            if near is near_x:
                field[near_at, i + 1] = near[i]
                field[far_at, i + 1] = far[i]
            else:
                field[i + 1, near_at] = near[i]
                field[i + 1, far_at] = far[i]

    def extend(edge, along_x, at, end, inner):
        @pl.when(edge)
        def _():
            for i in range(1, (by if along_x else bx) + 1):
                if along_x:
                    field[at, i] = 2.0 * field[end, i] - field[inner, i]
                else:
                    field[i, at] = 2.0 * field[i, end] - field[i, inner]

    extend(gx == 0, True, 0, 1, 2)
    extend(gx == lax.axis_size("gx") - 1, True, bx + 1, bx, bx - 1)
    extend(gy == 0, False, 0, 1, 2)
    extend(gy == lax.axis_size("gy") - 1, False, by + 1, by, by - 1)

    lane = iota(1)
    low = lane < NW
    turn = -1.0 + ((lane % NW).astype(jnp.float32) + 0.5) * (2.0 / NW)
    turn_up = turn > 0.0
    turn_rate = jnp.abs(turn) / HEAD_STEP
    turn_first = lane % NW == 0
    turn_last = lane % NW == NW - 1

    for part, start, x, y_start, length in runs(bx, by):

        def slopes(i, carry, part=part, start=start, x=x, y_start=y_start):
            y = y_start + i
            east_wind, north_wind = wind_at(wind, x, y)
            cells = load(field, x + 1, y + 1)
            for j in range(SLABS):
                c = cells[j]
                twice = c + c
                east = table[0, :, lanes(j)] + east_wind
                ahead = jnp.where(
                    east > 0.0, field[x + 2, y + 1, :, lanes(j)], field[x, y + 1, :, lanes(j)]
                )
                total = jnp.abs(east) * (ahead - c)
                north = table[1, :, lanes(j)] + north_wind
                ahead = jnp.where(
                    north > 0.0, field[x + 1, y + 2, :, lanes(j)], field[x + 1, y, :, lanes(j)]
                )
                total += jnp.abs(north) * (ahead - c)
                ahead = jnp.where(
                    turn_up, pltpu.roll(c, NTH - 1, axis=0), pltpu.roll(c, 1, axis=0)
                )
                total += turn_rate * (ahead - c)
                after = pltpu.roll(c, LANES - 1, axis=1)
                before = pltpu.roll(c, 1, axis=1)
                ahead = jnp.maximum(
                    jnp.where(turn_last, twice - before, after),
                    jnp.where(turn_first, twice - after, before),
                )
                total += (TURN_LIMIT / TURN_STEP) * (ahead - c)
                after, before = speed_sides(cells, j, low, twice)
                change = after - before
                total += (change * change) * (
                    0.25 / (SPEED_STEP * SPEED_STEP) / (2.0 * EFFORT_COST)
                )
                parts[part][start + i, :, lanes(j)] = total
            return carry

        walk(length, slopes, 0)

    for fetch in fetches:
        fetch.wait()
    if first:
        keeps = []
        for x in range(bx):
            for y in range(by):
                store(barrier[x], apart(load(raw, x, y), low), y)
            keeps.append(pltpu.make_async_copy(barrier[x], kept.at[x], sems.at[x]))
            keeps[-1].start()
        for keep in keeps:
            keep.wait()


def update_kernel(step, last, got, rate_row, steps_in, field_in, *refs):
    bx, by = field_in.shape[:2]
    parts, barrier, refs = refs[:5], refs[5 : 5 + bx], refs[5 + bx :]
    lane = lax.broadcasted_iota(jnp.int32, (1, LANES), 1)
    both = jnp.max(got[...], axis=0)
    gap = jnp.max(jnp.where(lane < NW, both, 0.0), keepdims=True)
    rate = jnp.max(jnp.where(lane < NW, 0.0, both), keepdims=True)
    top_slope = gap / SPEED_STEP
    time_step = COURANT / (rate + top_slope / (EFFORT_COST * SPEED_STEP))
    weight = jnp.broadcast_to(time_step, TILE)
    weight_scaled = jnp.broadcast_to(
        time_step * (top_slope / EFFORT_COST) * (0.5 / SPEED_STEP), TILE
    )
    steps = jnp.where(lane == step, time_step, steps_in[...])
    low = iota(1) < NW
    if last:
        value_out, steps_out, field_out, steps_here, sems = refs
    else:
        field_out, near_x, far_x, near_y, far_y, row, steps_out = refs
        steps_out[...] = steps

    copies = []
    if last:
        for i in range(ITERS):
            steps_here[i] = steps[0, i]
        copies.append(pltpu.make_async_copy(steps_here, steps_out, sems.at[0]))
        copies[0].start()
    peak = jnp.zeros(TILE, jnp.float32)
    for part, start, x, y_start, length in runs(bx, by):

        def update(i, peak, part=part, start=start, x=x, y_start=y_start):
            y = y_start + i
            old = load(field_in, x, y)
            cells = []
            for j in range(SLABS):
                twice = old[j] + old[j]
                after, before = speed_sides(old, j, low, twice)
                value = old[j] + weight * parts[part][start + i, :, lanes(j)]
                value += weight_scaled * ((after + before) - twice)
                cells.append(jnp.minimum(value, barrier[x][y, :, lanes(j)]))
            if last:
                store(field_out, together(cells, low), x, y)
                return peak
            store(field_out, cells, x, y)
            return speed_gap(peak, cells, low)

        peak = walk(length, update, peak)
        if last:
            ys = pl.ds(y_start, length)
            copies.append(
                pltpu.make_async_copy(
                    field_out.at[x, ys], value_out.at[x, ys], sems.at[len(copies)]
                )
            )
            copies[-1].start()
    if last:
        for copy in copies:
            copy.wait()
    else:
        row[...] = gap_row(peak, rate_row[...], low)
        fill_edges(field_out, near_x, far_x, near_y, far_y)


def hold(*arrays, space=pltpu.VMEM):
    return [pltpu.with_memory_space_constraint(a, space) for a in arrays]


def swap(cells, along, first):
    nx, ny = lax.axis_size("gx"), lax.axis_size("gy")
    pairs = []
    for x in range(nx):
        for y in range(ny):
            if along == "gx":
                if (x - first) % 2 == 0 and (x + 1 < nx or first):
                    pairs.append(((x, y), ((x + 1) % nx, y)))
            elif y >= first and (y - first) % 2 == 0 and y + 1 < ny:
                pairs.append(((x, y), (x, y + 1)))
    paired = {i for pair in pairs for i in pair}
    for x in range(0, nx - 1, 2):
        for y in range(ny):
            if not paired & {(x, y), (x + 1, y)}:
                pairs.append(((x, y), (x + 1, y)))
    links = [(i * ny + j, k * ny + m) for (i, j), (k, m) in pairs]
    return lax.ppermute(cells, ("gx", "gy"), links + [(j, i) for i, j in links])


def per_device(value_field, obstacle, drift_field):
    bx, by = value_field.shape[:2]
    cells = value_field.shape[2:]
    size = value_field.size
    devices = lax.axis_size("gx") * lax.axis_size("gy")

    def in_vmem(*shape):
        return pltpu.VMEM(shape, jnp.float32)

    block = in_vmem(bx, by, *cells)
    parts = [in_vmem(n, *cells) for n in part_sizes(bx, by)]
    edges = parts[:4]
    row = in_vmem(1, LANES)
    in_hbm = jax.ShapeDtypeStruct(value_field.shape, jnp.float32)
    vmem, _, hbm = (pl.BlockSpec(memory_space=m) for m in (pltpu.VMEM, pltpu.SMEM, pltpu.HBM))

    def call(kernel, outs, *, out_specs=None, ins, in_specs=None, scratch=(), aliases={}):
        return pl.pallas_call(
            kernel,
            out_shape=tuple(outs),
            in_specs=in_specs or [vmem] * len(ins),
            out_specs=out_specs or [vmem] * len(outs),
            scratch_shapes=scratch,
            input_output_aliases=aliases,
            compiler_params=pltpu.CompilerParams(vmem_limit_bytes=VMEM_LIMIT),
            cost_estimate=pl.CostEstimate(
                flops=40 * size, bytes_accessed=16 * size, transcendentals=0
            ),
        )(*ins)

    outs = [block, row, *edges, row, in_vmem(2, *cells), in_vmem(2, bx, by, LANES)]
    field, sent, near_x, far_x, near_y, far_y, rate_row, table, wind = call(
        first_kernel,
        outs,
        ins=hold(drift_field.transpose(0, 2, 1), value_field, space=pltpu.HBM),
        in_specs=[hbm, hbm],
        scratch=[
            pltpu.VMEM(value_field.shape, jnp.float32),
            pltpu.VMEM((bx, 2, by), jnp.float32),
            pltpu.SemaphoreType.DMA((bx + 1,)),
        ],
    )
    steps = jnp.zeros((1, LANES), jnp.float32)
    (limit,) = hold(obstacle, space=pltpu.HBM)
    padded = pltpu.VMEM((bx + 2, by + 2, *cells), jnp.float32)

    for step in range(ITERS):
        first, last = step == 0, step == ITERS - 1
        got_far_x = swap(far_x, "gx", 1)
        got_near_y = swap(near_y, "gy", 0)
        got_far_y = swap(far_y, "gy", 1)
        got_near_x = swap(near_x, "gx", 0)
        got_edges = [got_near_x, got_far_x, got_near_y, got_far_y]
        rows = jnp.broadcast_to(sent[None], (devices, 1, LANES))
        got = lax.all_to_all(rows, ("gx", "gy"), 0, 0)
        outs = [*parts, *[in_vmem(by, *cells)] * bx] + [pltpu.HBM(value_field.shape, jnp.float32)] * first
        ins = [*hold(table, wind, *got_edges, field), limit]
        result = call(
            functools.partial(slope_kernel, first),
            outs,
            out_specs=[vmem] * (5 + bx) + [hbm] * first,
            ins=ins,
            in_specs=[vmem] * 7 + [hbm],
            scratch=[padded]
            + [pltpu.VMEM(value_field.shape, jnp.float32)] * first
            + [pltpu.SemaphoreType.DMA((bx,))],
            aliases={2 + i: i for i in range(4)},
        )
        if first:
            *result, limit = result
            (limit,) = hold(limit, space=pltpu.HBM)
        ins = hold(got, rate_row, steps, field, *result)
        if last:
            return call(
                functools.partial(update_kernel, step, True),
                [in_hbm, jax.ShapeDtypeStruct((ITERS,), jnp.float32)],
                out_specs=[hbm, hbm],
                ins=ins,
                scratch=[
                    pltpu.VMEM(value_field.shape, jnp.float32),
                    pltpu.SMEM((ITERS,), jnp.float32),
                    pltpu.SemaphoreType.DMA((1 + len(runs(bx, by)),)),
                ],
            )
        field, near_x, far_x, near_y, far_y, sent, steps = call(
            functools.partial(update_kernel, step, False),
            [block, *edges, row, row],
            ins=ins,
            aliases={3: 0, **{4 + i: 1 + i for i in range(4)}},
        )


def solution(mesh):
    return jax.shard_map(
        per_device,
        mesh=mesh,
        in_specs=(P("gx", "gy", None, None), P("gx", "gy", None, None), P("gx", "gy", None)),
        out_specs=(P("gx", "gy", None, None), P()),
        check_vma=False,
    )
```

```python
import functools
import math

import jax
import jax.numpy as jnp
import numpy as np
from jax import lax
from jax.experimental import pallas as pl
from jax.experimental.pallas import tpu as pltpu
from jax.sharding import PartitionSpec as P


NTH = 8
NV = 16
NW = 64
ITERS = 4

SPACE_STEP = 0.5
SPEED_BASE = 1.0
SPEED_STEP = 0.2
TURN_LIMIT = 0.25
EFFORT_COST = 10.0
COURANT = 0.9
HEAD_STEP = 2.0 * math.pi / NTH
TURN_STEP = 2.0 / NW

LANES = 128
TILE = (NTH, LANES)
SLABS = NV * NW // LANES
VMEM_LIMIT = 24 * 1024 * 1024


def iota(dim):
    return lax.broadcasted_iota(jnp.int32, TILE, dim)


def lanes(j):
    return slice(j * LANES, (j + 1) * LANES)


def half_turn(c):
    return pltpu.roll(c, LANES // 2, axis=1)


def load(ref, *at):
    return [ref[(*at, slice(None), lanes(j))] for j in range(SLABS)]


def store(ref, cells, *at):
    for j in range(SLABS):
        ref[(*at, slice(None), lanes(j))] = cells[j]


def apart(cells, low):
    middle = SLABS // 2
    out = []
    for below, above in zip(cells[:middle], cells[middle:]):
        out += [jnp.where(low, below, half_turn(above)), jnp.where(low, half_turn(below), above)]
    return out


def together(cells, low):
    below = [jnp.where(low, c, half_turn(d)) for c, d in zip(cells[::2], cells[1::2])]
    above = [jnp.where(low, half_turn(c), d) for c, d in zip(cells[::2], cells[1::2])]
    return below + above


def speed_gap(peak, cells, low):
    for j in range(SLABS - 1):
        peak = jnp.maximum(peak, jnp.abs(cells[j + 1] - cells[j]))
    seam = jnp.abs(half_turn(cells[0]) - cells[-1])
    return jnp.maximum(peak, jnp.where(low, seam, 0.0))


def speed_sides(cells, j, low, twice):
    if j < SLABS - 1:
        after = cells[j + 1]
    else:
        after = jnp.where(low, half_turn(cells[0]), twice - cells[j - 1])
    if j:
        before = cells[j - 1]
    else:
        before = jnp.where(low, twice - cells[1], half_turn(cells[-1]))
    return after, before


def wind_at(wind, x, y):
    return wind[0, x, y : y + 1, :], wind[1, x, y : y + 1, :]


def gap_row(peak, rate_row, low):
    return jnp.where(low[:1], jnp.max(peak, keepdims=True), rate_row)


def part_sizes(bx, by):
    sizes = [by, by, bx, bx]
    return sizes + [bx * by - sum(sizes)]


def runs(bx, by):
    out, at = [], 0
    for part, size in enumerate(part_sizes(bx, by)):
        done = 0
        while done < size:
            x, y = divmod(at, by)
            length = min(size - done, by - y)
            out.append((part, done, x, y, length))
            done, at = done + length, at + length
    return out


def walk(length, body, carry):
    for i in range(length):
        carry = body(i, carry)
    return carry


def fill_edges(field, near_x, far_x, near_y, far_y):
    bx, by = field.shape[:2]
    for axis, size, near, far in (("gx", bx, near_x, far_x), ("gy", by, near_y, far_y)):
        even = lax.rem(lax.axis_index(axis), 2) == 0
        near_at = jnp.where(even, size - 1, 0)
        far_at = jnp.where(even, 0, size - 1)
        for i in range(near.shape[0]):
            near[i] = field[near_at, i] if axis == "gx" else field[i, near_at]
            far[i] = field[far_at, i] if axis == "gx" else field[i, far_at]


def first_kernel(drift_in, value, field, row, near_x, far_x, near_y, far_y, rate_out, table, wind, raw, drift, sems):
    bx, by = field.shape[:2]
    copies = [pltpu.make_async_copy(value.at[x], raw.at[x], sems.at[x]) for x in range(bx)]
    copies.append(pltpu.make_async_copy(drift_in, drift, sems.at[bx]))
    for copy in copies[-1:] + copies[:-1]:
        copy.start()
    low = iota(1) < NW
    heading = iota(0)
    cosine = jnp.zeros(TILE, jnp.float32)
    sine = jnp.zeros(TILE, jnp.float32)
    for a in range(NTH):
        angle = np.float32(a) * np.float32(HEAD_STEP)
        cosine = jnp.where(heading == a, np.cos(angle), cosine)
        sine = jnp.where(heading == a, np.sin(angle), sine)
    for j in range(SLABS):
        index = (j + SLABS * (iota(1) // NW)).astype(jnp.float32)
        speed = (SPEED_BASE + index * SPEED_STEP) * (1.0 / SPACE_STEP)
        table[0, :, lanes(j)] = cosine * speed
        table[1, :, lanes(j)] = sine * speed
    copies[bx].wait()
    diagonal = lax.broadcasted_iota(jnp.int32, (by, by), 0) == lax.broadcasted_iota(
        jnp.int32, (by, by), 1
    )
    for x in range(bx):
        for d in range(2):
            square = jnp.broadcast_to(drift[x, d : d + 1, :] * (1.0 / SPACE_STEP), (by, by))
            column = jnp.sum(jnp.where(diagonal, square, 0.0), axis=1, keepdims=True)
            wind[d, x] = jnp.broadcast_to(column, wind.shape[2:])

    moving = jnp.zeros(TILE, jnp.float32)
    for x in range(bx):

        def rate_of(y, peak, x=x):
            east, north = wind_at(wind, x, y)
            for j in (0, SLABS - 1):
                peak = jnp.maximum(
                    peak,
                    jnp.abs(table[0, :, lanes(j)] + east) + jnp.abs(table[1, :, lanes(j)] + north),
                )
            return peak

        moving = walk(by, rate_of, moving)
    turn = -1.0 + ((iota(1) % NW).astype(jnp.float32) + 0.5) * (2.0 / NW)
    turn_top = jnp.max(jnp.abs(turn), keepdims=True) / HEAD_STEP
    rate = jnp.max(moving, keepdims=True) + turn_top + TURN_LIMIT / TURN_STEP
    rate_row = jnp.broadcast_to(rate, (1, LANES))
    rate_out[...] = rate_row

    peak = jnp.zeros(TILE, jnp.float32)
    for x in range(bx):
        copies[x].wait()

        def gap_of(y, peak, x=x):
            cells = apart(load(raw, x, y), low)
            store(field, cells, x, y)
            return speed_gap(peak, cells, low)

        peak = walk(by, gap_of, peak)
    row[...] = gap_row(peak, rate_row, low)
    fill_edges(field, near_x, far_x, near_y, far_y)


def slope_kernel(first, table, wind, near_x, far_x, near_y, far_y, center, limit, *refs):
    parts, refs = refs[:5], refs[5:]
    bx, by = center.shape[:2]
    barrier, refs = refs[:bx], refs[bx:]
    if first:
        kept, field, raw, sems = refs
        targets = [raw.at[x] for x in range(bx)]
    else:
        field, sems = refs
        targets = barrier
    fetches = [pltpu.make_async_copy(limit.at[x], targets[x], sems.at[x]) for x in range(bx)]
    for fetch in fetches:
        fetch.start()
    gx, gy = lax.axis_index("gx"), lax.axis_index("gy")
    for x in range(bx):
        for y in range(by):
            field[x + 1, y + 1] = center[x, y]
    for index, size, near, far in ((gx, bx, near_x, far_x), (gy, by, near_y, far_y)):
        even = lax.rem(index, 2) == 0
        near_at = jnp.where(even, size + 1, 0)
        far_at = jnp.where(even, 0, size + 1)
        for i in range(near.shape[0]):
            if near is near_x:
                field[near_at, i + 1] = near[i]
                field[far_at, i + 1] = far[i]
            else:
                field[i + 1, near_at] = near[i]
                field[i + 1, far_at] = far[i]

    def extend(edge, along_x, at, end, inner):
        @pl.when(edge)
        def _():
            for i in range(1, (by if along_x else bx) + 1):
                if along_x:
                    field[at, i] = 2.0 * field[end, i] - field[inner, i]
                else:
                    field[i, at] = 2.0 * field[i, end] - field[i, inner]

    extend(gx == 0, True, 0, 1, 2)
    extend(gx == lax.axis_size("gx") - 1, True, bx + 1, bx, bx - 1)
    extend(gy == 0, False, 0, 1, 2)
    extend(gy == lax.axis_size("gy") - 1, False, by + 1, by, by - 1)

    lane = iota(1)
    low = lane < NW
    turn = -1.0 + ((lane % NW).astype(jnp.float32) + 0.5) * (2.0 / NW)
    turn_up = turn > 0.0
    turn_rate = jnp.abs(turn) / HEAD_STEP
    turn_first = lane % NW == 0
    turn_last = lane % NW == NW - 1

    keeps = []
    for part, start, x, y_start, length in runs(bx, by):

        def slopes(i, carry, part=part, start=start, x=x, y_start=y_start):
            y = y_start + i
            east_wind, north_wind = wind_at(wind, x, y)
            cells = load(field, x + 1, y + 1)
            for j in range(SLABS):
                c = cells[j]
                twice = c + c
                east = table[0, :, lanes(j)] + east_wind
                ahead = jnp.where(
                    east > 0.0, field[x + 2, y + 1, :, lanes(j)], field[x, y + 1, :, lanes(j)]
                )
                total = jnp.abs(east) * (ahead - c)
                north = table[1, :, lanes(j)] + north_wind
                ahead = jnp.where(
                    north > 0.0, field[x + 1, y + 2, :, lanes(j)], field[x + 1, y, :, lanes(j)]
                )
                total += jnp.abs(north) * (ahead - c)
                ahead = jnp.where(
                    turn_up, pltpu.roll(c, NTH - 1, axis=0), pltpu.roll(c, 1, axis=0)
                )
                total += turn_rate * (ahead - c)
                after = pltpu.roll(c, LANES - 1, axis=1)
                before = pltpu.roll(c, 1, axis=1)
                ahead = jnp.maximum(
                    jnp.where(turn_last, twice - before, after),
                    jnp.where(turn_first, twice - after, before),
                )
                total += (TURN_LIMIT / TURN_STEP) * (ahead - c)
                after, before = speed_sides(cells, j, low, twice)
                change = after - before
                total += (change * change) * (
                    0.25 / (SPEED_STEP * SPEED_STEP) / (2.0 * EFFORT_COST)
                )
                parts[part][start + i, :, lanes(j)] = total
            return carry

        if first and x == bx - 1 and y_start + length == by:
            for k in range(bx):
                fetches[k].wait()
                for y in range(by):
                    store(barrier[k], apart(load(raw, k, y), low), y)
                keeps.append(pltpu.make_async_copy(barrier[k], kept.at[k], sems.at[k]))
                keeps[-1].start()
        walk(length, slopes, 0)

    if not first:
        for fetch in fetches:
            fetch.wait()
    for keep in keeps:
        keep.wait()


def update_kernel(step, last, got, rate_row, steps_in, field_in, *refs):
    bx, by = field_in.shape[:2]
    parts, barrier, refs = refs[:5], refs[5 : 5 + bx], refs[5 + bx :]
    lane = lax.broadcasted_iota(jnp.int32, (1, LANES), 1)
    both = jnp.max(got[...], axis=0)
    gap = jnp.max(jnp.where(lane < NW, both, 0.0), keepdims=True)
    rate = jnp.max(jnp.where(lane < NW, 0.0, both), keepdims=True)
    top_slope = gap / SPEED_STEP
    time_step = COURANT / (rate + top_slope / (EFFORT_COST * SPEED_STEP))
    weight = jnp.broadcast_to(time_step, TILE)
    weight_scaled = jnp.broadcast_to(
        time_step * (top_slope / EFFORT_COST) * (0.5 / SPEED_STEP), TILE
    )
    steps = jnp.where(lane == step, time_step, steps_in[...])
    low = iota(1) < NW
    if last:
        value_out, steps_out, field_out, steps_here, sems = refs
    else:
        field_out, near_x, far_x, near_y, far_y, row, steps_out = refs
        steps_out[...] = steps

    copies = []
    peak = jnp.zeros(TILE, jnp.float32)
    for part, start, x, y_start, length in runs(bx, by):

        def update(i, peak, part=part, start=start, x=x, y_start=y_start):
            y = y_start + i
            old = load(field_in, x, y)
            cells = []
            for j in range(SLABS):
                twice = old[j] + old[j]
                after, before = speed_sides(old, j, low, twice)
                value = old[j] + weight * parts[part][start + i, :, lanes(j)]
                value += weight_scaled * ((after + before) - twice)
                cells.append(jnp.minimum(value, barrier[x][y, :, lanes(j)]))
            if last:
                store(field_out, together(cells, low), x, y)
                return peak
            store(field_out, cells, x, y)
            return speed_gap(peak, cells, low)

        peak = walk(length, update, peak)
        if last:
            ys = pl.ds(y_start, length)
            copies.append(
                pltpu.make_async_copy(
                    field_out.at[x, ys], value_out.at[x, ys], sems.at[len(copies)]
                )
            )
            copies[-1].start()
    if last:
        for i in range(ITERS):
            steps_here[i] = steps[0, i]
        copies.append(pltpu.make_async_copy(steps_here, steps_out, sems.at[len(copies)]))
        copies[-1].start()
        for copy in copies:
            copy.wait()
    else:
        row[...] = gap_row(peak, rate_row[...], low)
        fill_edges(field_out, near_x, far_x, near_y, far_y)


def hold(*arrays, space=pltpu.VMEM):
    return [pltpu.with_memory_space_constraint(a, space) for a in arrays]


def swap(cells, along, first):
    nx, ny = lax.axis_size("gx"), lax.axis_size("gy")
    pairs = []
    for x in range(nx):
        for y in range(ny):
            if along == "gx":
                if (x - first) % 2 == 0 and (x + 1 < nx or first):
                    pairs.append(((x, y), ((x + 1) % nx, y)))
            elif y >= first and (y - first) % 2 == 0 and y + 1 < ny:
                pairs.append(((x, y), (x, y + 1)))
    paired = {i for pair in pairs for i in pair}
    for x in range(0, nx - 1, 2):
        for y in range(ny):
            if not paired & {(x, y), (x + 1, y)}:
                pairs.append(((x, y), (x + 1, y)))
    links = [(i * ny + j, k * ny + m) for (i, j), (k, m) in pairs]
    return lax.ppermute(cells, ("gx", "gy"), links + [(j, i) for i, j in links])


def per_device(value_field, obstacle, drift_field):
    bx, by = value_field.shape[:2]
    cells = value_field.shape[2:]
    size = value_field.size
    devices = lax.axis_size("gx") * lax.axis_size("gy")

    def in_vmem(*shape):
        return pltpu.VMEM(shape, jnp.float32)

    block = in_vmem(bx, by, *cells)
    parts = [in_vmem(n, *cells) for n in part_sizes(bx, by)]
    edges = parts[:4]
    row = in_vmem(1, LANES)
    in_hbm = jax.ShapeDtypeStruct(value_field.shape, jnp.float32)
    vmem, _, hbm = (pl.BlockSpec(memory_space=m) for m in (pltpu.VMEM, pltpu.SMEM, pltpu.HBM))

    def call(kernel, outs, *, out_specs=None, ins, in_specs=None, scratch=(), aliases={}):
        return pl.pallas_call(
            kernel,
            out_shape=tuple(outs),
            in_specs=in_specs or [vmem] * len(ins),
            out_specs=out_specs or [vmem] * len(outs),
            scratch_shapes=scratch,
            input_output_aliases=aliases,
            compiler_params=pltpu.CompilerParams(vmem_limit_bytes=VMEM_LIMIT),
            cost_estimate=pl.CostEstimate(
                flops=40 * size, bytes_accessed=16 * size, transcendentals=0
            ),
        )(*ins)

    outs = [block, row, *edges, row, in_vmem(2, *cells), in_vmem(2, bx, by, LANES)]
    field, sent, near_x, far_x, near_y, far_y, rate_row, table, wind = call(
        first_kernel,
        outs,
        ins=hold(drift_field.transpose(0, 2, 1), value_field, space=pltpu.HBM),
        in_specs=[hbm, hbm],
        scratch=[
            pltpu.VMEM(value_field.shape, jnp.float32),
            pltpu.VMEM((bx, 2, by), jnp.float32),
            pltpu.SemaphoreType.DMA((bx + 1,)),
        ],
    )
    steps = jnp.zeros((1, LANES), jnp.float32)
    (limit,) = hold(obstacle, space=pltpu.HBM)
    padded = pltpu.VMEM((bx + 2, by + 2, *cells), jnp.float32)

    for step in range(ITERS):
        first, last = step == 0, step == ITERS - 1
        got_far_x = swap(far_x, "gx", 1)
        got_near_y = swap(near_y, "gy", 0)
        got_far_y = swap(far_y, "gy", 1)
        got_near_x = swap(near_x, "gx", 0)
        got_edges = [got_near_x, got_far_x, got_near_y, got_far_y]
        rows = jnp.broadcast_to(sent[None], (devices, 1, LANES))
        got = lax.all_to_all(rows, ("gx", "gy"), 0, 0)
        outs = [*parts, *[in_vmem(by, *cells)] * bx] + [pltpu.HBM(value_field.shape, jnp.float32)] * first
        ins = [*hold(table, wind, *got_edges, field), limit]
        result = call(
            functools.partial(slope_kernel, first),
            outs,
            out_specs=[vmem] * (5 + bx) + [hbm] * first,
            ins=ins,
            in_specs=[vmem] * 7 + [hbm],
            scratch=[padded]
            + [pltpu.VMEM(value_field.shape, jnp.float32)] * first
            + [pltpu.SemaphoreType.DMA((bx,))],
            aliases={2 + i: i for i in range(4)},
        )
        if first:
            *result, limit = result
            (limit,) = hold(limit, space=pltpu.HBM)
        ins = hold(got, rate_row, steps, field, *result)
        if last:
            return call(
                functools.partial(update_kernel, step, True),
                [in_hbm, jax.ShapeDtypeStruct((ITERS,), jnp.float32)],
                out_specs=[hbm, hbm],
                ins=ins,
                scratch=[
                    pltpu.VMEM(value_field.shape, jnp.float32),
                    pltpu.SMEM((ITERS,), jnp.float32),
                    pltpu.SemaphoreType.DMA((1 + len(runs(bx, by)),)),
                ],
            )
        field, near_x, far_x, near_y, far_y, sent, steps = call(
            functools.partial(update_kernel, step, False),
            [block, *edges, row, row],
            ins=ins,
            aliases={3: 0, **{4 + i: 1 + i for i in range(4)}},
        )


def solution(mesh):
    return jax.shard_map(
        per_device,
        mesh=mesh,
        in_specs=(P("gx", "gy", None, None), P("gx", "gy", None, None), P("gx", "gy", None)),
        out_specs=(P("gx", "gy", None, None), P()),
        check_vma=False,
    )
```
